32 devices in a mesh: group: 2 (over x), dp: 2 (over core), tensor: 8 (over z, y).
Axes of the slice: x: 2, y: 2, z: 4, core: 2. Of those that a mesh axis runs over, the one named last changes fastest.
Arguments:
- teacher_hidden: bfloat16 [1024, 8192], P(('group', 'dp'), 'tensor'), may hold values from -6 to 6
- teacher_gain: float32 [8192], P('tensor'), may hold values from 0.1 to 1.9
- project_weight: bfloat16 [8192, 3584], P('tensor'), may hold values from -0.0625 to 0.0625
- student_hidden: bfloat16 [1024, 3584], P(('group', 'dp', 'tensor')), may hold values from -6 to 6
- student_gain: float32 [3584], replicated, may hold values from 0.1 to 1.9
- gate_weight: bfloat16 [3584, 9472], P(('group', 'dp'), 'tensor'), may hold values from -0.09375 to 0.09375
- up_weight: bfloat16 [3584, 9472], P(('group', 'dp'), 'tensor'), may hold values from -0.09375 to 0.09375
- down_weight: bfloat16 [9472, 3584], P('tensor', ('group', 'dp')), may hold values from -0.0625 to 0.0625
- owner_map: int32 [64, 1], P(('group', 'dp')), may hold values from 0 to 3; in each aligned block of 16 rows (0 to 15, 16 to 31, ...) at most 8 rows name the same one
- token_ids: int32 [1024], P(('group', 'dp', 'tensor')), may hold values from 0 to 511
- token_counts: int32 [64], P(('group', 'dp')), may hold values from 1 to 16
- id_weight: float32 [512], replicated, may hold values from 0.25 to 4
Outputs:
- student_out: bfloat16 [4, 16, 32, 3584], P(('group', 'dp'), 'tensor')
- down_grad: float32 [3584, 9472], P(('group', 'dp'), 'tensor')
The draws below stay inside these ranges and needn't reach their ends.
Inputs may be any that keep to these rules, and one draw needn't show every extreme that they name: `owner_map`: of the 16 episodes of one index of group and dp (aligned blocks of 16 rows), at most 8 have the same owner; owner o is index o of group and dp in mesh order.
All inputs are finite; a program needn't handle non-finite values.
Results may differ from the reference program's by a relative error of at most 0.02.
Values may be sent and summed in bfloat16 or wider, within the bound.
A program may use at most 128 MiB of HBM per device.

```python
import math
import jax
import jax.numpy as jnp
import numpy as np
from jax import lax

DT = 8192
DS = 3584
FSW = 9472
REL_VOCAB = 512
EP_LEN = 16
EPI_DEV = 16
SLOTS = 4
EPISODES = 64
TOKENS = 1024
CAP = 8
RECV = 32
N_GROUP = 2
N_DP = 2
N_TENSOR = 8


def set_ends(values, own_key, low, high):
    longest = values.shape.index(max(values.shape))
    spots = []
    for shift in (0, 1):
        where = [jax.random.randint(jax.random.fold_in(own_key, axis), (), 0, length) for axis, length in enumerate(values.shape)]
        where[longest] = (where[longest] + shift) % values.shape[longest]
        spots.append(tuple(where))
    return values.at[spots[0]].set(low).at[spots[1]].set(high)


def level_of(rng, shape, split, least, largest):
    level, own = 1.0, jax.random.fold_in(rng, 6)
    for dim, blocks in split:
        draws = jnp.exp(jax.random.uniform(jax.random.fold_in(own, dim), (blocks,), jnp.float32, least / len(split), largest / len(split)))
        level = level * jnp.repeat(draws, shape[dim] // blocks).reshape([-1 if axis == dim else 1 for axis in range(len(shape))])
    return level


def rank_table(number_of, lean):
    weights = [(1 << 20) // math.isqrt(rank ** lean) + 1 for rank in range(1, number_of + 1)]
    scale = 1 + sum(weights) // (1 << 30)
    return np.cumsum(np.array([max(1, weight // scale) for weight in weights]))


def ranked(key, shape, amount, skew):
    table = rank_table(amount, skew)
    pick = jax.random.randint(jax.random.fold_in(key, 1), shape, 0, int(table[amount - 1]))
    rank = jnp.searchsorted(jnp.asarray(table, jnp.int32), pick, side="right")
    return jax.random.permutation(jax.random.fold_in(key, 2), amount)[rank].astype(jnp.int32)


def assign_block(stream_key, own, number, rows, amount, top, most, skew):
    ranking = jax.random.permutation(stream_key, amount)
    crowded, usual = portions_of(amount, rows * top, most, skew, True), portions_of(amount, rows * top, most, skew, False)
    places = jnp.arange(amount)

    def named(sizes, rotation):
        used = int((sizes > 0).sum())
        fixed = max(1, used // 4)
        passed = fixed + (places - fixed + rotation * (used - fixed)) % max(1, amount - fixed)
        return jnp.zeros((amount,), jnp.int32).at[ranking[jnp.where(places < fixed, places, passed)]].set(jnp.asarray(sizes, jnp.int32))

    sizes = jnp.where(number % 4 == 0, named(crowded, number // 4), named(usual, number - number // 4 - 1))
    mixed = jax.random.permutation(jax.random.fold_in(own, 3), amount)
    donor, taker = mixed[0:amount // 2 * 2:2], mixed[1:amount // 2 * 2:2]
    margin = jnp.minimum(sizes[donor] - 1, most - sizes[taker]) // 2
    margin = jnp.where((donor == ranking[0]) | (taker == ranking[0]) | (sizes[taker] == 0), 0, jnp.maximum(margin, 0))
    passed = jax.random.randint(jax.random.fold_in(own, 4), (amount // 2,), 0, 1 << 20) % (margin + 1)
    sizes = sizes.at[donor].add(-passed).at[taker].add(passed)
    members = jnp.searchsorted(jnp.cumsum(sizes), jnp.arange(rows * top), side="right").astype(jnp.int32)
    grid = members.reshape(top, rows).T
    grid = grid[jax.random.permutation(jax.random.fold_in(own, 1), rows)]
    rotation = jax.random.randint(jax.random.fold_in(own, 2), (rows, 1), 0, top)
    return jnp.take_along_axis(grid, (jnp.arange(top)[None, :] + rotation) % top, axis=1)


def portions_of(amount, total, limit, lean, full):
    weights = [(1 << 20) // math.isqrt(grade ** lean) + 1 for grade in range(1, amount + 1)]
    largest = limit if full else min(limit, max(-(-total // amount), total * weights[0] // sum(weights)))
    least = 1 if total - largest >= amount - 1 else 0
    given, spare = [largest] + [least] * (amount - 1), total - largest - least * (amount - 1)
    while spare > 0:
        movable = [i for i in range(1, amount) if given[i] < largest] or [i for i in range(1, amount) if given[i] < limit]
        pool, remaining = sum([weights[i] for i in movable]), spare
        for i in movable:
            more = min(limit - given[i], max(1, remaining * weights[i] // pool), spare)
            given[i] = given[i] + more
            spare = spare - more
    return np.array(given)


def centred(own_key, shape, spread, reach, cuts=(), held_as=jnp.bfloat16):
    entries = spread * jax.random.normal(own_key, shape, jnp.float32)
    if cuts:
        entries = entries * level_of(own_key, shape, cuts, -0.22, 0.18)
    return jnp.clip(entries, -reach, reach).astype(held_as)


def setup_inputs(seed: int = 0) -> dict:
    streams_of = jax.random.split(jax.random.key(seed), 13)
    teacher_hidden = centred(streams_of[0], (TOKENS, DT), 1.0, 6.0, ((0, 4), (1, 8)))
    teacher_gain = jnp.clip(1.0 + 0.18 * jax.random.normal(streams_of[1], (DT,), jnp.float32), 0.1, 1.9)
    project_weight = centred(streams_of[2], (DT, DS), DT ** -0.5, 0.0625, ((0, 8),))
    student_hidden = centred(streams_of[3], (TOKENS, DS), 1.0, 6.0, ((0, 32),))
    student_gain = jnp.clip(1.0 + 0.18 * jax.random.normal(streams_of[4], (DS,), jnp.float32), 0.1, 1.9)
    gate_weight = centred(streams_of[5], (DS, FSW), DS ** -0.5, 0.09375, ((0, 4), (1, 8)))
    up_weight = centred(streams_of[6], (DS, FSW), DS ** -0.5, 0.09375, ((0, 4), (1, 8)))
    down_weight = centred(streams_of[7], (FSW, DS), FSW ** -0.5, 0.0625, ((0, 8), (1, 4)))
    owner_map_keys = jax.random.split(jax.random.fold_in(streams_of[8], 1), EPISODES // EPI_DEV)
    owner_map_turns = jax.random.permutation(jax.random.fold_in(streams_of[8], 3), EPISODES // EPI_DEV)
    owner_map = jax.vmap(lambda own, number: assign_block(jax.random.fold_in(streams_of[8], 2), own, number, EPI_DEV, SLOTS, 1, CAP, 2))(owner_map_keys, owner_map_turns).reshape((EPISODES, 1))
    token_ids = set_ends(ranked(streams_of[9], (TOKENS,), REL_VOCAB, 2), jax.random.fold_in(streams_of[9], 3), 0, REL_VOCAB - 1).astype(jnp.int32)
    token_counts = set_ends(jax.random.randint(streams_of[10], (EPISODES,), 1, EP_LEN + 1), jax.random.fold_in(streams_of[10], 1), 1, EP_LEN).astype(jnp.int32)
    id_weight = jnp.clip(jnp.exp(jax.random.uniform(streams_of[11], (REL_VOCAB,), jnp.float32, math.log(0.25), math.log(4.0))), 0.25, 4.0)
    return dict(teacher_hidden=teacher_hidden, teacher_gain=teacher_gain, project_weight=project_weight, student_hidden=student_hidden, student_gain=student_gain, gate_weight=gate_weight, up_weight=up_weight, down_weight=down_weight, owner_map=owner_map, token_ids=token_ids, token_counts=token_counts, id_weight=id_weight)


EPSILON = 1e-06

def reference(teacher_hidden, teacher_gain, project_weight, student_hidden, student_gain, gate_weight, up_weight, down_weight, owner_map, token_ids, token_counts, id_weight):
    owners = N_GROUP * N_DP
    token_index = jnp.arange(TOKENS, dtype=jnp.int32)
    position = token_index // EPI_DEV % EP_LEN
    episode = token_index // (EP_LEN * EPI_DEV) * EPI_DEV + token_index % EPI_DEV
    token_weight = jnp.where(position < token_counts[episode], id_weight[token_ids], 0.0).astype(jnp.bfloat16)
    widened = teacher_hidden.astype(jnp.float32)
    inverse = lax.rsqrt(lax.optimization_barrier(jnp.mean(widened * widened, axis=1)) + EPSILON)
    scaled = (widened * teacher_gain[None, :]).astype(jnp.bfloat16)
    feature_block = DT // N_TENSOR

    def add_teacher(index, total):
        offset = (index * feature_block).astype(jnp.int32)
        columns = lax.dynamic_slice_in_dim(scaled, offset, feature_block, 1)
        weight_rows = lax.dynamic_slice_in_dim(project_weight, offset, feature_block, 0)
        partial_sum = jnp.dot(columns, weight_rows, preferred_element_type=jnp.float32).astype(jnp.bfloat16)
        return total + lax.optimization_barrier(partial_sum).astype(jnp.float32)
    summed = lax.fori_loop(0, N_TENSOR, add_teacher, jnp.zeros((TOKENS, DS), jnp.float32))
    projected = (summed * inverse[:, None]).astype(jnp.bfloat16)
    student_wide = student_hidden.astype(jnp.float32)
    rescale = lax.rsqrt(lax.optimization_barrier(jnp.mean(student_wide * student_wide, axis=1, keepdims=True)) + EPSILON)
    normed = (student_wide * rescale * student_gain[None, :]).astype(jnp.bfloat16)
    gate_sum = jnp.dot(normed, gate_weight, preferred_element_type=jnp.float32)
    up_sum = jnp.dot(normed, up_weight, preferred_element_type=jnp.float32)
    activated = (jax.nn.silu(gate_sum) * up_sum).astype(jnp.bfloat16)
    hidden_block = FSW // N_TENSOR

    def add_branch(index, total):
        offset = (index * hidden_block).astype(jnp.int32)
        columns = lax.dynamic_slice_in_dim(activated, offset, hidden_block, 1)
        weight_rows = lax.dynamic_slice_in_dim(down_weight, offset, hidden_block, 0)
        partial_sum = jnp.dot(columns, weight_rows, preferred_element_type=jnp.float32).astype(jnp.bfloat16)
        return total + lax.optimization_barrier(partial_sum).astype(jnp.float32)
    branch = lax.fori_loop(0, N_TENSOR, add_branch, jnp.zeros((TOKENS, DS), jnp.float32))
    predicted = student_wide + branch
    grad_rows = (token_weight.astype(jnp.float32)[:, None] * (predicted - projected.astype(jnp.float32)) / jnp.sqrt(jnp.float32(TOKENS))).astype(jnp.bfloat16)
    owner_list = owner_map[:, 0].reshape(owners, EPI_DEV)
    onehot = (owner_list[:, :, None] == jnp.arange(owners, dtype=jnp.int32)[None, None, :]).astype(jnp.int32)
    earlier = jnp.cumsum(onehot, axis=1) - onehot
    rank_list = lax.optimization_barrier(jnp.sum(earlier * onehot, axis=2))
    target = owner_list * CAP + rank_list
    wanted = jnp.arange(owners, dtype=jnp.int32)[:, None] * CAP + jnp.arange(CAP, dtype=jnp.int32)[None, :]
    matches = (target[None, :, None, :] == wanted[:, None, :, None]).astype(jnp.int32)
    found = lax.optimization_barrier(jnp.sum(matches, axis=3))
    chosen = lax.optimization_barrier(jnp.sum(matches * jnp.arange(EPI_DEV, dtype=jnp.int32)[None, None, None, :], axis=3))
    source_index = jnp.arange(owners, dtype=jnp.int32)[None, None, :, None]
    place_index = jnp.arange(EP_LEN, dtype=jnp.int32)[None, :, None, None]
    row_index = (source_index * EP_LEN + place_index) * EPI_DEV + chosen[:, None, :, :]
    row_index = jnp.where(found[:, None, :, :] > 0, row_index, TOKENS).astype(jnp.int32)
    row_index = row_index.reshape(owners, EP_LEN * owners * CAP)
    padded_out = jnp.concatenate([predicted.astype(jnp.bfloat16), jnp.zeros((1, DS), jnp.bfloat16)], axis=0)
    student_out = jnp.take(padded_out, row_index.reshape(-1), axis=0).reshape(owners, EP_LEN, RECV, DS)
    grad_padded = jnp.concatenate([grad_rows, jnp.zeros((1, DS), jnp.bfloat16)], axis=0)
    act_padded = jnp.concatenate([activated, jnp.zeros((1, FSW), jnp.bfloat16)], axis=0)

    def add_owner(index, total):
        chosen_rows = row_index[index]
        grad_part = jnp.take(grad_padded, chosen_rows, axis=0).astype(jnp.float32)
        act_part = jnp.take(act_padded, chosen_rows, axis=0).astype(jnp.float32)
        term = jnp.einsum('rc,rh->ch', grad_part, act_part)
        return total + lax.optimization_barrier(term.astype(jnp.bfloat16)).astype(jnp.float32)
    down_grad = lax.fori_loop(0, owners, add_owner, jnp.zeros((DS, FSW), jnp.float32))
    return (student_out, down_grad)
```

```python
import math

import jax
import jax.numpy as jnp
from jax import lax
from jax.sharding import PartitionSpec as P

EP_LEN = 16
EXTRA = 128
EPSILON = 1e-06
OWNER_AXES = ("group", "dp")


def exchange(blocks):
    return lax.all_to_all(blocks, OWNER_AXES, split_axis=0, concat_axis=0, tiled=True)


def by_columns(rows, owners):
    return rows.reshape(rows.shape[0], owners, -1).transpose(1, 0, 2)


def three_terms(values):
    high = lax.reduce_precision(values, 8, 7)
    rest = values - high
    middle = lax.reduce_precision(rest, 8, 7)
    return high, middle, rest - middle


def build_selector(owner_list, owners, capacity):
    onehot = (owner_list[:, :, None] == jnp.arange(owners, dtype=jnp.int32)).astype(jnp.int32)
    earlier = jnp.cumsum(onehot, axis=1) - onehot
    rank_list = jnp.sum(earlier * onehot, axis=2)
    target = owner_list * capacity + rank_list
    slots = jnp.arange(owners * capacity, dtype=jnp.int32)
    return (target[:, None, :] == slots[None, :, None]).astype(jnp.bfloat16)


def local(
    teacher_hidden,
    teacher_gain,
    project_weight,
    student_hidden,
    student_gain,
    gate_weight,
    up_weight,
    down_weight,
    owner_map,
    token_ids,
    token_counts,
    id_weight,
):
    owners = lax.axis_size("group") * lax.axis_size("dp")
    tensors = lax.axis_size("tensor")
    tensor_index = lax.axis_index("tensor")
    owner_index = lax.axis_index(OWNER_AXES)
    episodes = token_counts.shape[0]
    own_span = EP_LEN // tensors
    share = own_span * episodes
    capacity = max(2, 2 * episodes // owners)
    received = owners * capacity
    student_width = student_hidden.shape[1]
    width = student_width // owners
    tokens_all = EP_LEN * episodes * owners
    teacher_width = teacher_hidden.shape[1] * tensors

    id_rows = token_ids.reshape(own_span, episodes)
    looked = jnp.sum(
        jnp.where(
            id_rows[:, :, None] == jnp.arange(id_weight.shape[0], dtype=jnp.int32)[None, None, :],
            id_weight[None, None, :],
            0.0,
        ),
        axis=2,
    )
    position = tensor_index * own_span + jnp.arange(own_span, dtype=jnp.int32)[:, None]
    token_weight = jnp.where(position < token_counts[None, :], looked, 0.0).reshape(share, 1)

    own_rows = student_hidden.astype(jnp.float32)
    own_rescale = lax.rsqrt(jnp.mean(own_rows * own_rows, axis=1, keepdims=True) + EPSILON)
    owner_rows = jnp.tile(owner_map.astype(jnp.float32), (own_span, 1))
    extras = jnp.concatenate([token_weight, owner_rows, *three_terms(own_rescale)], axis=1)
    extras = jnp.pad(extras, ((0, 0), (0, EXTRA - extras.shape[1]))).astype(jnp.bfloat16)
    arrived = exchange(
        jnp.concatenate(
            [
                by_columns(student_hidden, owners),
                jnp.broadcast_to(extras[None], (owners, share, EXTRA)),
            ],
            axis=2,
        )
    )
    rows = owners * share
    student_block = arrived[:, :, :width].reshape(rows, width).astype(jnp.float32)
    facts = arrived[:, :, width:].astype(jnp.float32)
    weight_rows = facts[:, :, 0].reshape(rows, 1)
    owner_list = facts[:, :episodes, 1].astype(jnp.int32)
    rescale = (facts[:, :, 2] + facts[:, :, 3] + facts[:, :, 4]).reshape(rows, 1)
    gain = lax.dynamic_slice_in_dim(student_gain, owner_index * width, width, 0)
    normed = (student_block * rescale * gain[None, :]).astype(jnp.bfloat16)
    gathered = lax.all_gather(normed, "tensor", axis=0, tiled=True)

    widened = teacher_hidden.astype(jnp.float32)
    squares = jnp.sum(widened * widened, axis=1)
    scaled = (widened * teacher_gain[None, :]).astype(jnp.bfloat16)
    inverse = lax.rsqrt(lax.psum(squares, "tensor") / teacher_width + EPSILON)
    summed = lax.psum_scatter(
        jnp.dot(scaled, project_weight, preferred_element_type=jnp.float32).astype(jnp.bfloat16),
        "tensor",
        scatter_dimension=0,
        tiled=True,
    ).astype(jnp.float32)
    own_inverse = lax.dynamic_slice_in_dim(inverse, tensor_index * share, share, 0)
    projected = exchange(by_columns((summed * own_inverse[:, None]).astype(jnp.bfloat16), owners))

    hidden = gate_weight.shape[1]
    gate_part = jnp.dot(gathered, gate_weight, preferred_element_type=jnp.float32)
    up_part = jnp.dot(gathered, up_weight, preferred_element_type=jnp.float32)
    parts = jnp.stack(
        [
            gate_part.astype(jnp.bfloat16).reshape(owners, -1, hidden),
            up_part.astype(jnp.bfloat16).reshape(owners, -1, hidden),
        ],
        axis=1,
    )
    sums = lax.psum_scatter(parts, OWNER_AXES, scatter_dimension=0, tiled=True).astype(jnp.float32)
    activated = (jax.nn.silu(sums[0, 0]) * sums[0, 1]).astype(jnp.bfloat16)
    act_all = lax.all_gather(activated, OWNER_AXES, axis=0, tiled=True)
    branch = jnp.dot(act_all, down_weight, preferred_element_type=jnp.float32)
    branch_local = lax.psum_scatter(
        branch.astype(jnp.bfloat16), "tensor", scatter_dimension=0, tiled=True
    ).astype(jnp.float32)
    predicted = student_block + branch_local

    difference = predicted - projected.reshape(rows, width).astype(jnp.float32)
    grad_block = (weight_rows * difference * (1.0 / math.sqrt(tokens_all))).astype(jnp.bfloat16)
    grad_all = lax.all_gather(grad_block, "tensor", axis=0, tiled=True)
    down_grad = jnp.einsum("rc,rh->ch", grad_all, act_all, preferred_element_type=jnp.float32)

    selector = build_selector(owner_list, owners, capacity)
    picked = jnp.einsum(
        "sre,spef->sprf",
        selector,
        predicted.astype(jnp.bfloat16).reshape(owners, own_span, episodes, width),
        preferred_element_type=jnp.float32,
    ).astype(jnp.bfloat16)
    outgoing = picked.reshape(owners, own_span, owners, capacity, width).transpose(2, 1, 0, 3, 4)
    incoming = exchange(outgoing.reshape(owners, own_span, received, width))
    student_out = incoming.transpose(1, 2, 0, 3).reshape(1, own_span, received, student_width)
    return (student_out, down_grad)


def solution(mesh):
    in_specs = (
        P(("group", "dp"), "tensor"),
        P("tensor"),
        P("tensor", None),
        P(("group", "dp", "tensor"), None),
        P(),
        P(("group", "dp"), "tensor"),
        P(("group", "dp"), "tensor"),
        P("tensor", ("group", "dp")),
        P(("group", "dp"), None),
        P(("group", "dp", "tensor")),
        P(("group", "dp")),
        P(),
    )
    out_specs = (P(("group", "dp"), "tensor", None, None), P(("group", "dp"), "tensor"))
    return jax.shard_map(local, mesh=mesh, in_specs=in_specs, out_specs=out_specs, check_vma=False)
```
